512 devices in a mesh: dom: 32 (over x, y, z_hi), lat: 16 (over z_lo, core).
Axes of the slice: x: 4, y: 4, z: 16 (z_hi: 2, z_lo: 8; z = z_hi * 8 + z_lo), core: 2. Of those that a mesh axis runs over, the one named last changes fastest.
Arguments:
- states: float32 [3, 64, 256, 1024], P(None, 'dom', 'lat'), may hold values from -3 to 3
- stir_noise: float32 [2, 64, 256, 1024], P(None, 'dom', 'lat'), may hold values from -1.2 to 1.2
- ancestors: int32 [2, 32, 2], replicated, may hold values from 0 to 3, as said below
Outputs:
- filtered: float32 [3, 64, 256, 1024], P(None, 'dom', 'lat')
The draws below stay inside these ranges and needn't reach their ends.
Inputs may be any that keep to these rules, and one draw needn't show every extreme that they name: An entry from 2 upward names a particle of the preceding island on the loop; in every row ancestors[c, i, :] exactly one entry is 2 or more.
All inputs are finite; a program needn't handle non-finite values.
Results may differ from the reference program's by a relative error of at most 0.0003.
Values sent between devices are 32-bit elements; how exact they have to be, the bound alone decides.
A program may use at most 64 MiB of HBM per device.

```python
import jax
import jax.numpy as jnp
from jax import lax

P_ISL = 2
NX = 1024
STEPS = 2
FILTER_ROUNDS = 2
ISLANDS = 32
PARTICLES = 64
NY = 256


def draw_ancestors(key, part):
    key_order = jax.random.fold_in(key, 11)
    key_source = jax.random.fold_in(key, 23)
    shape = (FILTER_ROUNDS, ISLANDS, P_ISL)
    scores = jax.random.randint(key_order, shape, 0, 1 << 20) * P_ISL + jnp.arange(P_ISL, dtype=jnp.int32)
    ranking = jnp.argsort(jnp.argsort(scores, axis=-1, stable=True), axis=-1, stable=True)
    foreign = ranking < P_ISL // 2
    donor_particle = jax.random.randint(key_source, shape, 0, P_ISL)
    first_island = (jnp.arange(ISLANDS, dtype=jnp.int32) == 0)[None, :, None]
    donor_particle = jnp.where(first_island, jnp.where(foreign, P_ISL - 1, 0), donor_particle)
    return jnp.where(foreign, P_ISL + donor_particle, donor_particle).astype(jnp.int32)


def levels(key, shape, split, least, top_value):
    def one(dim, parts):
        heights = jax.random.uniform(jax.random.fold_in(jax.random.fold_in(key, 6), dim), (parts,), jnp.float32, least / len(split), top_value / len(split))
        return jnp.repeat(jnp.exp(heights), shape[dim] // parts).reshape((-1,) + (1,) * (len(shape) - dim - 1))

    factor_of = one(*split[0])
    for cut in split[1:]:
        factor_of = factor_of * one(*cut)
    return factor_of


def scatter_about(rng, extent, scale, limit, cuts=(), kind=jnp.bfloat16):
    array = scale * jax.random.normal(rng, extent, jnp.float32)
    if cuts:
        array = array * levels(rng, extent, cuts, -0.22, 0.18)
    return jnp.clip(array, -limit, limit).astype(kind)


def setup_inputs(seed: int = 0) -> dict:
    key_list = jax.random.split(jax.random.key(seed), 4)
    return {
        "states": scatter_about(key_list[0], (3, PARTICLES, NY, NX), 0.5, 3.0, ((1, 32), (2, 16)), jnp.float32),
        "stir_noise": scatter_about(key_list[1], (FILTER_ROUNDS, PARTICLES, NY, NX), 0.2, 1.2, ((1, 32), (2, 16)), jnp.float32),
        "ancestors": draw_ancestors(jax.random.fold_in(key_list[3], 71), 0),
    }


time_step = 0.2
viscosity = 0.05
rotation = 0.3


def eastward(field_amount):
    return jnp.roll(field_amount, -1, axis=-1)


def westward(field_amount):
    return jnp.roll(field_amount, 1, axis=-1)


def slope_x(field_amount):
    return (eastward(field_amount) - westward(field_amount)) * 0.5


def slope_y(field_amount):
    return (field_amount[..., 2:, :] - field_amount[..., :-2, :]) * 0.5


def laplace(field_amount, middle):
    return eastward(middle) + westward(middle) + field_amount[..., 2:, :] + field_amount[..., :-2, :] - 4.0 * middle


def tendency(padded, coriolis):
    height = padded[0]
    zonal = padded[1]
    northward = padded[2]
    height_mid = height[..., 1:-1, :]
    zonal_mid = zonal[..., 1:-1, :]
    north_mid = northward[..., 1:-1, :]
    column_depth = 1.0 + height
    flux_east = column_depth[..., 1:-1, :] * zonal_mid
    flux_north = column_depth * northward
    tend_height = -slope_x(flux_east) - slope_y(flux_north) + viscosity * laplace(height, height_mid)
    tend_zonal = (-zonal_mid * slope_x(zonal_mid) - north_mid * slope_y(zonal) + coriolis * north_mid
                  - slope_x(height_mid) + viscosity * laplace(zonal, zonal_mid))
    tend_north = (-zonal_mid * slope_x(north_mid) - north_mid * slope_y(northward) - coriolis * zonal_mid
                  - slope_y(height) + viscosity * laplace(northward, north_mid))
    return jnp.stack([tend_height, tend_zonal, tend_north])


def coriolis_rows(start_row, row_count, all_rows):
    row_index = start_row + jnp.arange(row_count, dtype=jnp.int32)
    return (rotation * (2.0 * (row_index.astype(jnp.float32) + 0.5) / all_rows - 1.0))[:, None]


def pad_rows(fields):
    return jnp.pad(fields, ((0, 0), (0, 0), (1, 1), (0, 0)))


def heun_step(fields, coriolis):
    first_section = fields + time_step * tendency(pad_rows(fields), coriolis)
    return 0.5 * (fields + first_section + time_step * tendency(pad_rows(first_section), coriolis))


def reference(states, stir_noise, ancestors):
    islands = ancestors.shape[1]
    per_island = ancestors.shape[2]
    total_rows = states.shape[2]
    coriolis = coriolis_rows(0, total_rows, total_rows)
    island_groups = states.reshape(3, islands, per_island, total_rows, -1).transpose(1, 0, 2, 3, 4)
    for cycle_idx in range(FILTER_ROUNDS):
        driving_term = stir_noise[cycle_idx].reshape(islands, per_island, total_rows, -1)

        def predicted_state(paired_inputs):
            island_state, island_noise = paired_inputs
            for step_idx in range(STEPS):
                island_state = heun_step(island_state, coriolis)
            return jnp.concatenate([island_state[0:1] + island_noise[None], island_state[1:]], axis=0)

        island_groups = lax.map(predicted_state, (island_groups, driving_term))
        cycle_parents = ancestors[cycle_idx]

        def resample(island):
            own_state = island_groups[island]
            before = island_groups[(island - 1) % islands]
            pooled = jnp.concatenate([own_state, before], axis=1)
            return jnp.take(pooled, cycle_parents[island], axis=1)

        island_groups = lax.map(resample, jnp.arange(islands, dtype=jnp.int32))
    return island_groups.transpose(1, 0, 2, 3, 4).reshape(states.shape)
```

```python
import functools

import jax
import jax.numpy as jnp
from jax import lax
from jax.experimental import pallas as pl
from jax.experimental.pallas import tpu as pltpu
from jax.sharding import PartitionSpec as P

MESH = pl.DeviceIdType.MESH
DT = 0.2
HALF = 0.5 * DT
NU = 0.05 * DT
ROT = 0.3
W = 1024
HOPS = 8


def terms(h, u, v, hs, us, vs, cor):
    he, hw, hn, hb = hs
    ue, uw, un, ub = us
    ve, vw, vn, vb = vs
    dux = ue - uw
    dvy = vn - vb
    bh = (he * ue - hw * uw) + (hn * vn - hb * vb) + (dux + dvy)
    bu = u * dux + v * (un - ub) + (he - hw)
    bv = u * (ve - vw) + v * dvy + (hn - hb)
    lh = (he + hw) + (hn + hb)
    lu = (ue + uw) + (un + ub)
    lv = (ve + vw) + (vn + vb)
    keep = 1.0 - 4.0 * NU
    return (
        h * keep + NU * lh - HALF * bh,
        u * keep + NU * lu - HALF * bu + cor * v,
        v * keep + NU * lv - HALF * bv - cor * u,
    )


def stage_tile(src, old, cor, t):
    r = 8 * t
    sub = lax.broadcasted_iota(jnp.int32, (8, W), 0)
    mid, shifts = [], []
    for f in range(3):
        c = src[f, pl.ds(r, 8), :]
        nxt = src[f, pl.ds(r + 8, 8), :]
        prv = src[f, pl.ds(r - 8, 8), :]
        mid.append(c)
        shifts.append(
            (
                pltpu.roll(c, W - 1, 1),
                pltpu.roll(c, 1, 1),
                jnp.where(sub == 7, pltpu.roll(nxt, 7, 0), pltpu.roll(c, 7, 0)),
                jnp.where(sub == 0, pltpu.roll(prv, 1, 0), pltpu.roll(c, 1, 0)),
            )
        )
    cr = jnp.broadcast_to(cor[pl.ds(r, 8), 0:1], (8, W))
    new = terms(*mid, *shifts, cr)
    if old is None:
        return new
    return tuple(0.5 * (old[f, pl.ds(r, 8), :] + new[f]) for f in range(3))


def kernel(
    islands, lats, anc, states, noise, out, xe, ne, n1, a, b, cor, own, foh, ring, byp, ovm,
    lsem, hsend, hrecv, rsend, rrecv, bsend, brecv, osem,
):
    dom, lat = lax.axis_index("dom"), lax.axis_index("lat")
    columns = islands // 2
    half = lats // 2
    depth = 2 * half
    xy, core = dom // 2, lat % 2
    z = (dom % 2) * half + lat // 2

    def at(xy_, z_):
        return (xy_ * 2 + z_ // half, (z_ % half) * 2 + core)

    zs = ((z + 1) % depth, (z + depth - 1) % depth)
    nxt_xy, prv_xy = (xy + 1) % columns, (xy + columns - 1) % columns
    low = (z < half).astype(jnp.int32)

    def hop(d, n):
        zt = zs[d]
        if n < HOPS:
            return at(xy, zt)
        return at((xy + (zt < half).astype(jnp.int32)) % columns, zt)

    loads = [
        pltpu.make_async_copy(states, xe.at[:, :, pl.ds(8, 16)], lsem.at[0]),
        pltpu.make_async_copy(noise.at[0], ne.at[:, pl.ds(8, 16)], lsem.at[1]),
        pltpu.make_async_copy(noise.at[1], n1, lsem.at[2]),
    ]
    for c in loads:
        c.start()

    barrier = pltpu.get_barrier_semaphore()
    from_xy = (xy + columns - low) % columns
    for d in range(2):
        pl.semaphore_signal(barrier, 1, device_id=at(xy, zs[d]), device_id_type=MESH)
        pl.semaphore_signal(barrier, 1, device_id=at(from_xy, zs[d]), device_id_type=MESH)
    pl.semaphore_signal(barrier, 1, device_id=at(prv_xy, z), device_id_type=MESH)

    @pl.when(lat > 0)
    def _():
        pl.semaphore_signal(barrier, 1, device_id=(dom, lat - 1), device_id_type=MESH)

    @pl.when(lat < lats - 1)
    def _():
        pl.semaphore_signal(barrier, 1, device_id=(dom, lat + 1), device_id_type=MESH)

    row = lax.broadcasted_iota(jnp.int32, (48, 128), 0) - 16 + lat * 16
    cor[...] = (DT * ROT) * (2.0 * (row.astype(jnp.float32) + 0.5) / (lats * 16) - 1.0)

    @pl.when(lat == 0)
    def _():
        xe[:, :, pl.ds(0, 8), :] = jnp.zeros((3, 2, 8, W), jnp.float32)
        ne[:, pl.ds(0, 8), :] = jnp.zeros((2, 8, W), jnp.float32)

    @pl.when(lat == lats - 1)
    def _():
        xe[:, :, pl.ds(24, 8), :] = jnp.zeros((3, 2, 8, W), jnp.float32)
        ne[:, pl.ds(24, 8), :] = jnp.zeros((2, 8, W), jnp.float32)

    for c in loads:
        c.wait()
    pl.semaphore_wait(
        barrier, 5 + (lat > 0).astype(jnp.int32) + (lat < lats - 1).astype(jnp.int32)
    )

    def halo(d):
        s, t = (8, 24) if d == 0 else (16, 0)
        dev = (dom, lat - 1) if d == 0 else (dom, lat + 1)
        return [
            pltpu.make_async_remote_copy(
                xe.at[:, :, pl.ds(s, 8)], xe.at[:, :, pl.ds(t, 8)], hsend.at[d, 0], hrecv.at[d, 0],
                device_id=dev, device_id_type=MESH,
            ),
            pltpu.make_async_remote_copy(
                ne.at[:, pl.ds(s, 8)], ne.at[:, pl.ds(t, 8)], hsend.at[d, 1], hrecv.at[d, 1],
                device_id=dev, device_id_type=MESH,
            ),
        ]

    @pl.when(lat > 0)
    def _():
        for c in halo(0):
            c.start()

    @pl.when(lat < lats - 1)
    def _():
        for c in halo(1):
            c.start()

    def row_of(c, island):
        j0, j1 = anc[c, island, 0], anc[c, island, 1]
        keep = (j0 >= 2).astype(jnp.int32)
        return keep, jnp.where(j0 >= 2, j1, j0), jnp.where(j0 >= 2, j0, j1) - 2

    nxt, prv = (dom + 1) % islands, (dom + islands - 1) % islands
    o0, a0, _ = row_of(0, dom)
    o0p, _, _ = row_of(0, prv)
    _, _, b0n = row_of(0, nxt)
    o1, a1, b1 = row_of(1, dom)
    _, _, b1n = row_of(1, nxt)

    @pl.when(lat < lats - 1)
    def _():
        for c in halo(0):
            c.wait_recv()

    @pl.when(lat > 0)
    def _():
        for c in halo(1):
            c.wait_recv()

    def masked(t, val):
        if t == 1:
            return jnp.where(lat > 0, val, 0.0)
        if t == 4:
            return jnp.where(lat < lats - 1, val, 0.0)
        return val

    def forecast():
        def step(_, carry):
            for src, dst, old in ((a, b, None), (b, a, a)):
                for t in range(1, 5):
                    new = stage_tile(src, old, cor, t)
                    for f in range(3):
                        dst[f, pl.ds(8 * t, 8), :] = masked(t, new[f])
            return carry

        lax.fori_loop(0, 2, step, 0)

    def twice(pick):
        for t in range(1, 5):
            r = 8 * t
            for f in range(3):
                a[f, pl.ds(r, 8), :] = jnp.where(
                    pick == 1, xe[f, 1, pl.ds(r - 8, 8), :], xe[f, 0, pl.ds(r - 8, 8), :]
                )
        forecast()
        for t in range(1, 5):
            r = 8 * t
            add = jnp.where(pick == 1, ne[1, pl.ds(r - 8, 8), :], ne[0, pl.ds(r - 8, 8), :])
            a[0, pl.ds(r, 8), :] = masked(t, a[0, pl.ds(r, 8), :] + add)
        forecast()

    def send(d, n, k):
        src = own.at[d, k] if n == 1 else ring.at[d, n - 2, k]
        return pltpu.make_async_remote_copy(
            src, ring.at[d, n - 1, k], rsend.at[d, n - 1, k], rrecv.at[d, n - 1, k],
            device_id=hop(d, n), device_id_type=MESH,
        )

    def pass_on(d):
        return pltpu.make_async_remote_copy(
            own.at[d, pl.ds(0, 3)], byp.at[d], bsend.at[d], brecv.at[d],
            device_id=at(nxt_xy, z), device_id_type=MESH,
        )

    twice(b0n)
    for f in range(3):
        for d in range(2):
            own[d, f] = a[f, pl.ds(16 + 8 * d, 8), :]
            send(d, 1, f).start()
    for d in range(2):
        pass_on(d).start()

    twice(a0)
    for d in range(2):
        rows = pl.ds(8 * d, 8)
        fh = a[0, pl.ds(16 + 8 * d, 8), :]
        foh[d] = fh
        own[d, 3] = jnp.where(b1n == o0, fh, 0.0) + jnp.where(b1n == 1, n1[1, rows, :], n1[0, rows, :])
        send(d, 1, 3).start()
    for f in range(1, 3):
        for d in range(2):
            own[d, 3 + f] = a[f, pl.ds(16 + 8 * d, 8), :]
            send(d, 1, 3 + f).start()

    for n in range(2, HOPS + 1):
        for k in range(6):
            for d in range(2):
                send(d, n - 1, k).wait_recv()
                send(d, n, k).start()

    @pl.when(lat > 0)
    def _():
        for c in halo(0):
            c.wait_send()

    @pl.when(lat < lats - 1)
    def _():
        for c in halo(1):
            c.wait_send()

    for d in range(2):
        pass_on(d).wait()
    for n in range(1, HOPS):
        for k in range(6):
            for d in range(2):
                send(d, n, k).wait_send()

    last = HOPS - 1

    def put(f, d, va, vb):
        rows = pl.ds(8 * d, 8)
        ovm[f, 0, rows, :] = jnp.where(o1 == 0, va, vb)
        ovm[f, 1, rows, :] = jnp.where(o1 == 0, vb, va)

    for k in range(3):
        for d in range(2):
            send(d, HOPS, k).wait_recv()
    for f in range(3):
        for d in range(2):
            rows = pl.ds(8 * d, 8)
            mine = foh[d] if f == 0 else own[d, 3 + f]
            va = jnp.where(a1 == o0, mine, ring[d, last, f])
            if f == 0:
                va = va + jnp.where(a1 == 1, n1[1, rows, :], n1[0, rows, :])
            send(d, HOPS, 3 + f).wait_recv()
            arrived = ring[d, last, 3 + f]
            if f == 0:
                vb = arrived + jnp.where(b1 == o0p, 0.0, byp[d, 0])
            else:
                vb = jnp.where(b1 == o0p, arrived, byp[d, f])
            put(f, d, va, vb)
        pltpu.make_async_copy(ovm.at[f], out.at[f], osem.at[f]).start()
    for k in range(6):
        for d in range(2):
            send(d, HOPS, k).wait_send()
    for f in range(3):
        pltpu.make_async_copy(ovm.at[f], out.at[f], osem.at[f]).wait()


def solution(mesh):
    islands, lats = mesh.shape["dom"], mesh.shape["lat"]

    def body(states, stir_noise, ancestors):
        f32 = jnp.float32
        dma = pltpu.SemaphoreType.DMA
        return pl.pallas_call(
            functools.partial(kernel, islands, lats),
            out_shape=jax.ShapeDtypeStruct(states.shape, f32),
            in_specs=[
                pl.BlockSpec(memory_space=pltpu.SMEM),
                pl.BlockSpec(memory_space=pl.ANY),
                pl.BlockSpec(memory_space=pl.ANY),
            ],
            out_specs=pl.BlockSpec(memory_space=pl.ANY),
            scratch_shapes=[
                pltpu.VMEM((3, 2, 32, W), f32),
                pltpu.VMEM((2, 32, W), f32),
                pltpu.VMEM((2, 16, W), f32),
                pltpu.VMEM((3, 48, W), f32),
                pltpu.VMEM((3, 48, W), f32),
                pltpu.VMEM((48, 128), f32),
                pltpu.VMEM((2, 6, 8, W), f32),
                pltpu.VMEM((2, 8, W), f32),
                pltpu.VMEM((2, HOPS, 6, 8, W), f32),
                pltpu.VMEM((2, 3, 8, W), f32),
                pltpu.VMEM((3, 2, 16, W), f32),
                dma((3,)),
                dma((2, 2)),
                dma((2, 2)),
                dma((2, HOPS, 6)),
                dma((2, HOPS, 6)),
                dma((2,)),
                dma((2,)),
                dma((3,)),
            ],
            compiler_params=pltpu.CompilerParams(collective_id=0, has_side_effects=True),
            name="filter_ring",
        )(ancestors, states, stir_noise)

    spec = P(None, "dom", "lat", None)
    return jax.shard_map(body, mesh=mesh, in_specs=(spec, spec, P()), out_specs=spec, check_vma=False)
```

```python
import functools

import jax
import jax.numpy as jnp
from jax import lax
from jax.experimental import pallas as pl
from jax.experimental.pallas import tpu as pltpu
from jax.sharding import PartitionSpec as P

MESH = pl.DeviceIdType.MESH
DT = 0.2
HALF = 0.5 * DT
NU = 0.05 * DT
ROT = 0.3
W = 1024
HOPS = 8
SIDE = 4


def terms(h, u, v, hs, us, vs, cor):
    he, hw, hn, hb = hs
    ue, uw, un, ub = us
    ve, vw, vn, vb = vs
    dux = ue - uw
    dvy = vn - vb
    bh = (he * ue - hw * uw) + (hn * vn - hb * vb) + (dux + dvy)
    bu = u * dux + v * (un - ub) + (he - hw)
    bv = u * (ve - vw) + v * dvy + (hn - hb)
    lh = (he + hw) + (hn + hb)
    lu = (ue + uw) + (un + ub)
    lv = (ve + vw) + (vn + vb)
    keep = 1.0 - 4.0 * NU
    return (
        h * keep + NU * lh - HALF * bh,
        u * keep + NU * lu - HALF * bu + cor * v,
        v * keep + NU * lv - HALF * bv - cor * u,
    )


def stage_tile(src, old, cor, t):
    r = 8 * t
    sub = lax.broadcasted_iota(jnp.int32, (8, W), 0)
    mid, shifts = [], []
    for f in range(3):
        c = src[f, pl.ds(r, 8), :]
        nxt = src[f, pl.ds(r + 8, 8), :]
        prv = src[f, pl.ds(r - 8, 8), :]
        mid.append(c)
        shifts.append(
            (
                pltpu.roll(c, W - 1, 1),
                pltpu.roll(c, 1, 1),
                jnp.where(sub == 7, pltpu.roll(nxt, 7, 0), pltpu.roll(c, 7, 0)),
                jnp.where(sub == 0, pltpu.roll(prv, 1, 0), pltpu.roll(c, 1, 0)),
            )
        )
    cr = jnp.broadcast_to(cor[pl.ds(r, 8), 0:1], (8, W))
    new = terms(*mid, *shifts, cr)
    if old is None:
        return new
    return tuple(0.5 * (old[f, pl.ds(r, 8), :] + new[f]) for f in range(3))


def kernel(
    islands, lats, parents, states, noise, out, anc, xr, n0, xs, n1, a, b, cor, own, foh, ring, byp,
    lsem, hsend, hrecv, rsend, rrecv, bsend, brecv,
):
    dom, lat = lax.axis_index("dom"), lax.axis_index("lat")
    columns = islands // 2
    half = lats // 2
    depth = 2 * half
    xy, core = dom // 2, lat % 2
    z = (dom % 2) * half + lat // 2

    def at(xy_, z_):
        return (xy_ * 2 + z_ // half, (z_ % half) * 2 + core)

    zs = ((z + 1) % depth, (z + depth - 1) % depth)
    nxt_xy, prv_xy = (xy + 1) % columns, (xy + columns - 1) % columns
    side = SIDE
    x, y = xy // side, xy % side
    east = x * side + (y + 1) % side
    west = x * side + (y + side - 1) % side
    over = (xy + side) % columns
    under = (xy + columns - side) % columns

    def hop(d, n):
        origin = (z + depth - (n - 1)) % depth if d == 0 else (z + n - 1) % depth
        high = origin // half
        to = xy
        if n == 3:
            to = high * east + (1 - high) * xy
        if n == 5:
            wrap = high * (y == 0).astype(jnp.int32)
            to = wrap * over + (1 - wrap) * xy
        return at(to, zs[d])

    loads = [
        pltpu.make_async_copy(states, xr, lsem.at[0]),
        pltpu.make_async_copy(noise.at[0], n0, lsem.at[1]),
        pltpu.make_async_copy(noise.at[1], n1, lsem.at[2]),
        pltpu.make_async_copy(parents, anc, lsem.at[3]),
    ]
    for c in loads:
        c.start()

    barrier = pltpu.get_barrier_semaphore()
    for d in range(2):
        for col in (xy, west, under):
            pl.semaphore_signal(barrier, 1, device_id=at(col, zs[d]), device_id_type=MESH)
    pl.semaphore_signal(barrier, 1, device_id=at(prv_xy, z), device_id_type=MESH)

    @pl.when(lat > 0)
    def _():
        pl.semaphore_signal(barrier, 1, device_id=(dom, lat - 1), device_id_type=MESH)

    @pl.when(lat < lats - 1)
    def _():
        pl.semaphore_signal(barrier, 1, device_id=(dom, lat + 1), device_id_type=MESH)

    row = lax.broadcasted_iota(jnp.int32, (48, 128), 0) - 16 + lat * 16
    cor[...] = (DT * ROT) * (2.0 * (row.astype(jnp.float32) + 0.5) / (lats * 16) - 1.0)

    @pl.when(lat == 0)
    def _():
        xs[:, :, pl.ds(0, 8), :] = jnp.zeros((2, 4, 8, W), jnp.float32)

    @pl.when(lat == lats - 1)
    def _():
        xs[:, :, pl.ds(24, 8), :] = jnp.zeros((2, 4, 8, W), jnp.float32)

    for c in loads:
        c.wait()
    def row_of(c, island):
        j0, j1 = anc[c, 0, island], anc[c, 1, island]
        keep = (j0 >= 2).astype(jnp.int32)
        return keep, jnp.where(j0 >= 2, j1, j0), jnp.where(j0 >= 2, j0, j1) - 2

    nxt, prv = (dom + 1) % islands, (dom + islands - 1) % islands
    o0, a0, _ = row_of(0, dom)
    o0p, _, _ = row_of(0, prv)
    _, _, b0n = row_of(0, nxt)
    o1, a1, b1 = row_of(1, dom)
    _, _, b1n = row_of(1, nxt)

    def choose(p, pick, rows):
        for f in range(3):
            xs[p, f, pl.ds(8 + rows, 8), :] = jnp.where(
                pick == 1, xr[f, 1, pl.ds(rows, 8), :], xr[f, 0, pl.ds(rows, 8), :]
            )
        xs[p, 3, pl.ds(8 + rows, 8), :] = jnp.where(pick == 1, n0[1, pl.ds(rows, 8), :], n0[0, pl.ds(rows, 8), :])

    for p, pick in ((0, b0n), (1, a0)):
        for rows in (0, 8):
            choose(p, pick, rows)

    pl.semaphore_wait(
        barrier, 7 + (lat > 0).astype(jnp.int32) + (lat < lats - 1).astype(jnp.int32)
    )

    def halo(d, p):
        s, t = (8, 24) if d == 0 else (16, 0)
        return pltpu.make_async_remote_copy(
            xs.at[p, :, pl.ds(s, 8)], xs.at[p, :, pl.ds(t, 8)], hsend.at[d, p], hrecv.at[d, p],
            device_id=(dom, lat - 1) if d == 0 else (dom, lat + 1), device_id_type=MESH,
        )

    for p in range(2):
        @pl.when(lat > 0)
        def _():
            halo(0, p).start()

        @pl.when(lat < lats - 1)
        def _():
            halo(1, p).start()

    def arrived_halo(p):
        @pl.when(lat < lats - 1)
        def _():
            halo(0, p).wait_recv()

        @pl.when(lat > 0)
        def _():
            halo(1, p).wait_recv()

    def masked(t, val):
        if t == 1:
            return jnp.where(lat > 0, val, 0.0)
        if t == 4:
            return jnp.where(lat < lats - 1, val, 0.0)
        return val

    def forecast():
        def step(_, carry):
            for src, dst, old in ((a, b, None), (b, a, a)):
                for t in range(1, 5):
                    new = stage_tile(src, old, cor, t)
                    for f in range(3):
                        dst[f, pl.ds(8 * t, 8), :] = masked(t, new[f])
            return carry

        lax.fori_loop(0, 2, step, 0)

    def twice(p):
        arrived_halo(p)
        for t in range(1, 5):
            r = 8 * t
            for f in range(3):
                a[f, pl.ds(r, 8), :] = xs[p, f, pl.ds(r - 8, 8), :]
        forecast()
        for t in range(1, 5):
            r = 8 * t
            a[0, pl.ds(r, 8), :] = masked(t, a[0, pl.ds(r, 8), :] + xs[p, 3, pl.ds(r - 8, 8), :])
        forecast()

    def send(d, n, k):
        src = own.at[d, k] if n == 1 else ring.at[d, n - 2, k]
        return pltpu.make_async_remote_copy(
            src, ring.at[d, n - 1, k], rsend.at[d, n - 1, k], rrecv.at[d, n - 1, k],
            device_id=hop(d, n), device_id_type=MESH,
        )

    def pass_on(d):
        return pltpu.make_async_remote_copy(
            own.at[d, pl.ds(0, 3)], byp.at[d], bsend.at[d], brecv.at[d],
            device_id=at(nxt_xy, z), device_id_type=MESH,
        )

    twice(0)
    for f in range(3):
        for d in range(2):
            own[d, f] = a[f, pl.ds(16 + 8 * d, 8), :]
            send(d, 1, f).start()
    for d in range(2):
        pass_on(d).start()

    twice(1)
    for d in range(2):
        rows = pl.ds(8 * d, 8)
        fh = a[0, pl.ds(16 + 8 * d, 8), :]
        foh[d] = fh
        own[d, 3] = jnp.where(b1n == o0, fh, 0.0) + jnp.where(b1n == 1, n1[1, rows, :], n1[0, rows, :])
        send(d, 1, 3).start()
    for f in range(1, 3):
        for d in range(2):
            own[d, 3 + f] = a[f, pl.ds(16 + 8 * d, 8), :]
            send(d, 1, 3 + f).start()

    for n in range(2, HOPS + 1):
        for k in range(6):
            for d in range(2):
                send(d, n - 1, k).wait_recv()
                send(d, n, k).start()

    @pl.when(lat > 0)
    def _():
        for p in range(2):
            halo(0, p).wait_send()

    @pl.when(lat < lats - 1)
    def _():
        for p in range(2):
            halo(1, p).wait_send()

    for d in range(2):
        pass_on(d).wait()
    for n in range(1, HOPS):
        for k in range(6):
            for d in range(2):
                send(d, n, k).wait_send()

    last = HOPS - 1

    def put(f, d, va, vb):
        rows = pl.ds(8 * d, 8)
        out[f, 0, rows, :] = jnp.where(o1 == 0, va, vb)
        out[f, 1, rows, :] = jnp.where(o1 == 0, vb, va)

    for k in range(3):
        for d in range(2):
            send(d, HOPS, k).wait_recv()
    for f in range(3):
        for d in range(2):
            rows = pl.ds(8 * d, 8)
            mine = foh[d] if f == 0 else own[d, 3 + f]
            va = jnp.where(a1 == o0, mine, ring[d, last, f])
            if f == 0:
                va = va + jnp.where(a1 == 1, n1[1, rows, :], n1[0, rows, :])
            send(d, HOPS, 3 + f).wait_recv()
            arrived = ring[d, last, 3 + f]
            if f == 0:
                vb = arrived + jnp.where(b1 == o0p, 0.0, byp[d, 0])
            else:
                vb = jnp.where(b1 == o0p, arrived, byp[d, f])
            put(f, d, va, vb)
    for k in range(6):
        for d in range(2):
            send(d, HOPS, k).wait_send()


def solution(mesh):
    islands, lats = mesh.shape["dom"], mesh.shape["lat"]

    def body(states, stir_noise, ancestors):
        f32 = jnp.float32
        dma = pltpu.SemaphoreType.DMA
        return pl.pallas_call(
            functools.partial(kernel, islands, lats),
            out_shape=jax.ShapeDtypeStruct(states.shape, f32),
            in_specs=[
                pl.BlockSpec(memory_space=pltpu.HBM),
                pl.BlockSpec(memory_space=pltpu.HBM),
                pl.BlockSpec(memory_space=pltpu.HBM),
            ],
            out_specs=pl.BlockSpec(memory_space=pltpu.VMEM),
            scratch_shapes=[
                pltpu.SMEM((2, 2, islands), jnp.int32),
                pltpu.VMEM((3, 2, 16, W), f32),
                pltpu.VMEM((2, 16, W), f32),
                pltpu.VMEM((2, 4, 32, W), f32),
                pltpu.VMEM((2, 16, W), f32),
                pltpu.VMEM((3, 48, W), f32),
                pltpu.VMEM((3, 48, W), f32),
                pltpu.VMEM((48, 128), f32),
                pltpu.VMEM((2, 6, 8, W), f32),
                pltpu.VMEM((2, 8, W), f32),
                pltpu.VMEM((2, HOPS, 6, 8, W), f32),
                pltpu.VMEM((2, 3, 8, W), f32),
                dma((4,)),
                dma((2, 2)),
                dma((2, 2)),
                dma((2, HOPS, 6)),
                dma((2, HOPS, 6)),
                dma((2,)),
                dma((2,)),
            ],
            compiler_params=pltpu.CompilerParams(collective_id=0, has_side_effects=True, vmem_limit_bytes=20 * 2**20),
            name="filter_ring",
        )(*(pltpu.with_memory_space_constraint(v, pltpu.HBM) for v in (jnp.transpose(ancestors, (0, 2, 1)), states, stir_noise)))

    spec = P(None, "dom", "lat", None)
    return jax.shard_map(body, mesh=mesh, in_specs=(spec, spec, P()), out_specs=spec, check_vma=False)
```

```python
import functools

import jax
import jax.numpy as jnp
from jax import lax
from jax.experimental import pallas as pl
from jax.experimental.pallas import tpu as pltpu
from jax.sharding import PartitionSpec as P

MESH = pl.DeviceIdType.MESH
DT = 0.2
HALF = 0.5 * DT
NU = 0.05 * DT
DEPTH = HALF * HALF
REST = (DEPTH, 0.0, 0.0)
ROT = 0.3
W = 1024
HOPS = 8
SIDE = 4


def terms(h, u, v, hs, us, vs, cor):
    he, hw, hn, hb = hs
    ue, uw, un, ub = us
    ve, vw, vn, vb = vs
    keep = 1.0 - 4.0 * NU
    lh = (he + hw) + (hn + hb)
    lu = (ue + uw) + (un + ub)
    lv = (ve + vw) + (vn + vb)
    return (
        h * keep + NU * lh - ((he * ue - hw * uw) + (hn * vn - hb * vb)),
        u * (keep - (ue - uw)) + v * (cor - (un - ub)) + (NU * lu - (he - hw)),
        v * (keep - (vn - vb)) - u * (cor + (ve - vw)) + (NU * lv - (hn - hb)),
    )


def stage_tile(src, old, cor, t):
    r = 8 * t
    sub = lax.broadcasted_iota(jnp.int32, (8, W), 0)
    mid, shifts = [], []
    for f in range(3):
        c = src[f, pl.ds(r, 8), :]
        nxt = src[f, pl.ds(r + 8, 8), :]
        prv = src[f, pl.ds(r - 8, 8), :]
        mid.append(c)
        shifts.append(
            (
                pltpu.roll(c, W - 1, 1),
                pltpu.roll(c, 1, 1),
                pltpu.roll(jnp.where(sub == 0, nxt, c), 7, 0),
                pltpu.roll(jnp.where(sub == 7, prv, c), 1, 0),
            )
        )
    cr = jnp.broadcast_to(cor[pl.ds(r, 8), 0:1], (8, W))
    new = terms(*mid, *shifts, cr)
    if old is None:
        return new
    return tuple(0.5 * (old[f, pl.ds(r, 8), :] + new[f]) for f in range(3))


def kernel(
    islands, lats, parents, states, noise, out, anc, xr, n0, xs, n1, a, b, cor, own, foh, ring, byp,
    lsem, hsend, hrecv, rsend, rrecv, bsend, brecv,
):
    dom, lat = lax.axis_index("dom"), lax.axis_index("lat")
    columns = islands // 2
    half = lats // 2
    depth = 2 * half
    xy, core = dom // 2, lat % 2
    z = (dom % 2) * half + lat // 2

    def at(xy_, z_):
        return (xy_ * 2 + z_ // half, (z_ % half) * 2 + core)

    zs = ((z + 1) % depth, (z + depth - 1) % depth)
    nxt_xy, prv_xy = (xy + 1) % columns, (xy + columns - 1) % columns
    side = SIDE
    x, y = xy // side, xy % side
    east = x * side + (y + 1) % side
    west = x * side + (y + side - 1) % side
    over = (xy + side) % columns
    under = (xy + columns - side) % columns

    def hop(d, n):
        origin = (z + depth - (n - 1)) % depth if d == 0 else (z + n - 1) % depth
        high = origin // half
        to = xy
        if n == 3:
            to = high * east + (1 - high) * xy
        if n == 5:
            wrap = high * (y == 0).astype(jnp.int32)
            to = wrap * over + (1 - wrap) * xy
        return at(to, zs[d])

    loads = [
        pltpu.make_async_copy(states, xr, lsem.at[0]),
        pltpu.make_async_copy(noise.at[0], n0, lsem.at[1]),
        pltpu.make_async_copy(noise.at[1], n1, lsem.at[2]),
        pltpu.make_async_copy(parents, anc, lsem.at[3]),
    ]
    for c in loads:
        c.start()

    barrier = pltpu.get_barrier_semaphore()
    for d in range(2):
        for col in (xy, west, under):
            pl.semaphore_signal(barrier, 1, device_id=at(col, zs[d]), device_id_type=MESH)
    pl.semaphore_signal(barrier, 1, device_id=at(prv_xy, z), device_id_type=MESH)

    @pl.when(lat > 0)
    def _():
        pl.semaphore_signal(barrier, 1, device_id=(dom, lat - 1), device_id_type=MESH)

    @pl.when(lat < lats - 1)
    def _():
        pl.semaphore_signal(barrier, 1, device_id=(dom, lat + 1), device_id_type=MESH)

    row = lax.broadcasted_iota(jnp.int32, (48, 128), 0) - 16 + lat * 16
    cor[...] = (DT * ROT) * (2.0 * (row.astype(jnp.float32) + 0.5) / (lats * 16) - 1.0)

    @pl.when(lat == 0)
    def _():
        xs[:, :, pl.ds(0, 8), :] = jnp.zeros((2, 4, 8, W), jnp.float32)
        xs[:, 0, pl.ds(0, 8), :] = jnp.full((2, 8, W), DEPTH, jnp.float32)

    @pl.when(lat == lats - 1)
    def _():
        xs[:, :, pl.ds(24, 8), :] = jnp.zeros((2, 4, 8, W), jnp.float32)
        xs[:, 0, pl.ds(24, 8), :] = jnp.full((2, 8, W), DEPTH, jnp.float32)

    for c in loads:
        c.wait()
    def row_of(c, island):
        j0, j1 = anc[c, 0, island], anc[c, 1, island]
        keep = (j0 >= 2).astype(jnp.int32)
        return keep, jnp.where(j0 >= 2, j1, j0), jnp.where(j0 >= 2, j0, j1) - 2

    nxt, prv = (dom + 1) % islands, (dom + islands - 1) % islands
    o0, a0, _ = row_of(0, dom)
    o0p, _, _ = row_of(0, prv)
    _, _, b0n = row_of(0, nxt)
    o1, a1, b1 = row_of(1, dom)
    _, _, b1n = row_of(1, nxt)

    def choose(p, pick, rows):
        for f in range(3):
            raw = jnp.where(pick == 1, xr[f, 1, pl.ds(rows, 8), :], xr[f, 0, pl.ds(rows, 8), :])
            xs[p, f, pl.ds(8 + rows, 8), :] = raw * HALF if f else DEPTH + raw * DEPTH
        add = jnp.where(pick == 1, n0[1, pl.ds(rows, 8), :], n0[0, pl.ds(rows, 8), :])
        xs[p, 3, pl.ds(8 + rows, 8), :] = add * DEPTH

    for p, pick in ((0, b0n), (1, a0)):
        for rows in (0, 8):
            choose(p, pick, rows)

    pl.semaphore_wait(
        barrier, 7 + (lat > 0).astype(jnp.int32) + (lat < lats - 1).astype(jnp.int32)
    )

    def halo(d, p):
        s, t = (8, 24) if d == 0 else (16, 0)
        return pltpu.make_async_remote_copy(
            xs.at[p, :, pl.ds(s, 8)], xs.at[p, :, pl.ds(t, 8)], hsend.at[d, p], hrecv.at[d, p],
            device_id=(dom, lat - 1) if d == 0 else (dom, lat + 1), device_id_type=MESH,
        )

    for p in range(2):
        @pl.when(lat > 0)
        def _():
            halo(0, p).start()

        @pl.when(lat < lats - 1)
        def _():
            halo(1, p).start()

    def arrived_halo(p):
        @pl.when(lat < lats - 1)
        def _():
            halo(0, p).wait_recv()

        @pl.when(lat > 0)
        def _():
            halo(1, p).wait_recv()

    def masked(t, val, f):
        if t == 1:
            return jnp.where(lat > 0, val, REST[f])
        if t == 4:
            return jnp.where(lat < lats - 1, val, REST[f])
        return val

    def section(src, dst, old, tiles):
        for t in tiles:
            new = stage_tile(src, old, cor, t)
            for f in range(3):
                dst[f, pl.ds(8 * t, 8), :] = masked(t, new[f], f)

    def forecast(last):
        every = range(1, 5)
        section(a, b, None, every)
        section(b, a, a, every)
        section(a, b, None, every)
        section(b, a, a, range(2, 4) if last else every)

    def twice(p):
        arrived_halo(p)
        for t in range(1, 5):
            r = 8 * t
            for f in range(3):
                a[f, pl.ds(r, 8), :] = xs[p, f, pl.ds(r - 8, 8), :]
        forecast(False)
        for t in range(1, 5):
            r = 8 * t
            a[0, pl.ds(r, 8), :] = masked(t, a[0, pl.ds(r, 8), :] + xs[p, 3, pl.ds(r - 8, 8), :], 0)
        forecast(True)

    def send(d, n, k):
        src = own.at[d, k] if n == 1 else ring.at[d, n - 2, k]
        return pltpu.make_async_remote_copy(
            src, ring.at[d, n - 1, k], rsend.at[d, n - 1, k], rrecv.at[d, n - 1, k],
            device_id=hop(d, n), device_id_type=MESH,
        )

    def pass_on(d):
        return pltpu.make_async_remote_copy(
            own.at[d, pl.ds(0, 3)], byp.at[d], bsend.at[d], brecv.at[d],
            device_id=at(nxt_xy, z), device_id_type=MESH,
        )

    twice(0)
    for f in range(3):
        for d in range(2):
            own[d, f] = a[f, pl.ds(16 + 8 * d, 8), :]
            send(d, 1, f).start()
    for d in range(2):
        pass_on(d).start()

    twice(1)
    for d in range(2):
        rows = pl.ds(8 * d, 8)
        fh = a[0, pl.ds(16 + 8 * d, 8), :]
        foh[d] = fh
        own[d, 3] = jnp.where(b1n == o0, fh, 0.0) + DEPTH * jnp.where(b1n == 1, n1[1, rows, :], n1[0, rows, :])
        send(d, 1, 3).start()
    for f in range(1, 3):
        for d in range(2):
            own[d, 3 + f] = a[f, pl.ds(16 + 8 * d, 8), :]
            send(d, 1, 3 + f).start()

    for n in range(2, HOPS + 1):
        for k in range(6):
            for d in range(2):
                send(d, n - 1, k).wait_recv()
                send(d, n, k).start()

    @pl.when(lat > 0)
    def _():
        for p in range(2):
            halo(0, p).wait_send()

    @pl.when(lat < lats - 1)
    def _():
        for p in range(2):
            halo(1, p).wait_send()

    for d in range(2):
        pass_on(d).wait()
    for n in range(1, HOPS):
        for k in range(6):
            for d in range(2):
                send(d, n, k).wait_send()

    last = HOPS - 1

    def plain(f, v):
        return v * (1.0 / HALF) if f else v * (1.0 / DEPTH) - 1.0

    def put(f, d, va, vb):
        rows = pl.ds(8 * d, 8)
        out[f, 0, rows, :] = jnp.where(o1 == 0, va, vb)
        out[f, 1, rows, :] = jnp.where(o1 == 0, vb, va)

    for k in range(3):
        for d in range(2):
            send(d, HOPS, k).wait_recv()
    for f in range(3):
        for d in range(2):
            rows = pl.ds(8 * d, 8)
            mine = foh[d] if f == 0 else own[d, 3 + f]
            va = jnp.where(a1 == o0, mine, ring[d, last, f])
            if f == 0:
                va = va + DEPTH * jnp.where(a1 == 1, n1[1, rows, :], n1[0, rows, :])
            send(d, HOPS, 3 + f).wait_recv()
            arrived = ring[d, last, 3 + f]
            if f == 0:
                vb = arrived + jnp.where(b1 == o0p, 0.0, byp[d, 0])
            else:
                vb = jnp.where(b1 == o0p, arrived, byp[d, f])
            put(f, d, plain(f, va), plain(f, vb))
    for k in range(6):
        for d in range(2):
            send(d, HOPS, k).wait_send()


def solution(mesh):
    islands, lats = mesh.shape["dom"], mesh.shape["lat"]

    def body(states, stir_noise, ancestors):
        f32 = jnp.float32
        dma = pltpu.SemaphoreType.DMA
        return pl.pallas_call(
            functools.partial(kernel, islands, lats),
            out_shape=jax.ShapeDtypeStruct(states.shape, f32),
            in_specs=[
                pl.BlockSpec(memory_space=pltpu.HBM),
                pl.BlockSpec(memory_space=pltpu.HBM),
                pl.BlockSpec(memory_space=pltpu.HBM),
            ],
            out_specs=pl.BlockSpec(memory_space=pltpu.VMEM),
            scratch_shapes=[
                pltpu.SMEM((2, 2, islands), jnp.int32),
                pltpu.VMEM((3, 2, 16, W), f32),
                pltpu.VMEM((2, 16, W), f32),
                pltpu.VMEM((2, 4, 32, W), f32),
                pltpu.VMEM((2, 16, W), f32),
                pltpu.VMEM((3, 48, W), f32),
                pltpu.VMEM((3, 48, W), f32),
                pltpu.VMEM((48, 128), f32),
                pltpu.VMEM((2, 6, 8, W), f32),
                pltpu.VMEM((2, 8, W), f32),
                pltpu.VMEM((2, HOPS, 6, 8, W), f32),
                pltpu.VMEM((2, 3, 8, W), f32),
                dma((4,)),
                dma((2, 2)),
                dma((2, 2)),
                dma((2, HOPS, 6)),
                dma((2, HOPS, 6)),
                dma((2,)),
                dma((2,)),
            ],
            compiler_params=pltpu.CompilerParams(collective_id=0, has_side_effects=True, vmem_limit_bytes=20 * 2**20),
            name="filter_ring",
        )(*(pltpu.with_memory_space_constraint(v, pltpu.HBM) for v in (jnp.transpose(ancestors, (0, 2, 1)), states, stir_noise)))

    spec = P(None, "dom", "lat", None)
    return jax.shard_map(body, mesh=mesh, in_specs=(spec, spec, P()), out_specs=spec, check_vma=False)
```

```python
import functools

import jax
import jax.numpy as jnp
from jax import lax
from jax.experimental import pallas as pl
from jax.experimental.pallas import tpu as pltpu
from jax.sharding import PartitionSpec as P

MESH = pl.DeviceIdType.MESH
DT = 0.2
HALF = 0.5 * DT
NU = 0.05 * DT
DEPTH = HALF * HALF
REST = (DEPTH, 0.0, 0.0)
ROT = 0.3
W = 1024
HOPS = 8
SIDE = 4


def terms(h, u, v, hs, us, vs, cor):
    he, hw, hn, hb = hs
    ue, uw, un, ub = us
    ve, vw, vn, vb = vs
    keep = 1.0 - 4.0 * NU
    lh = (he + hw) + (hn + hb)
    lu = (ue + uw) + (un + ub)
    lv = (ve + vw) + (vn + vb)
    return (
        h * keep + NU * lh - ((he * ue - hw * uw) + (hn * vn - hb * vb)),
        u * (keep - (ue - uw)) + v * (cor - (un - ub)) + (NU * lu - (he - hw)),
        v * (keep - (vn - vb)) - u * (cor + (ve - vw)) + (NU * lv - (hn - hb)),
    )


def stage_tile(src, old, cor, t):
    r = 8 * t
    sub = lax.broadcasted_iota(jnp.int32, (8, W), 0)
    mid, shifts = [], []
    for f in range(3):
        c = src[f, pl.ds(r, 8), :]
        nxt = src[f, pl.ds(r + 8, 8), :]
        prv = src[f, pl.ds(r - 8, 8), :]
        mid.append(c)
        shifts.append(
            (
                pltpu.roll(c, W - 1, 1),
                pltpu.roll(c, 1, 1),
                pltpu.roll(jnp.where(sub == 0, nxt, c), 7, 0),
                pltpu.roll(jnp.where(sub == 7, prv, c), 1, 0),
            )
        )
    cr = jnp.broadcast_to(cor[pl.ds(r, 8), 0:1], (8, W))
    new = terms(*mid, *shifts, cr)
    if old is None:
        return new
    return tuple(0.5 * (old[f, pl.ds(r, 8), :] + new[f]) for f in range(3))


def kernel(
    islands, lats, parents, states, noise, out, anc, xr, n0, xs, n1, a, b, cor, own, foh, ring, byp,
    lsem, hsend, hrecv, rsend, rrecv, bsend, brecv,
):
    dom, lat = lax.axis_index("dom"), lax.axis_index("lat")
    columns = islands // 2
    half = lats // 2
    depth = 2 * half
    xy, core = dom // 2, lat % 2
    z = (dom % 2) * half + lat // 2

    def at(xy_, z_):
        return (xy_ * 2 + z_ // half, (z_ % half) * 2 + core)

    zs = ((z + 1) % depth, (z + depth - 1) % depth)
    nxt_xy, prv_xy = (xy + 1) % columns, (xy + columns - 1) % columns
    side = SIDE
    x, y = xy // side, xy % side
    east = x * side + (y + 1) % side
    west = x * side + (y + side - 1) % side
    over = (xy + side) % columns
    under = (xy + columns - side) % columns

    def hop(d, n):
        origin = (z + depth - (n - 1)) % depth if d == 0 else (z + n - 1) % depth
        high = origin // half
        to = xy
        if n == 4:
            to = high * east + (1 - high) * xy
        if n == 6:
            wrap = high * (y == 0).astype(jnp.int32)
            to = wrap * over + (1 - wrap) * xy
        return at(to, zs[d])

    loads = [
        pltpu.make_async_copy(states, xr, lsem.at[0]),
        pltpu.make_async_copy(noise.at[0], n0, lsem.at[1]),
        pltpu.make_async_copy(noise.at[1], n1, lsem.at[2]),
        pltpu.make_async_copy(parents, anc, lsem.at[3]),
    ]
    for c in loads:
        c.start()

    barrier = pltpu.get_barrier_semaphore()
    for d in range(2):
        for col in (xy, west, under):
            pl.semaphore_signal(barrier, 1, device_id=at(col, zs[d]), device_id_type=MESH)
    pl.semaphore_signal(barrier, 1, device_id=at(prv_xy, z), device_id_type=MESH)

    @pl.when(lat > 0)
    def _():
        pl.semaphore_signal(barrier, 1, device_id=(dom, lat - 1), device_id_type=MESH)

    @pl.when(lat < lats - 1)
    def _():
        pl.semaphore_signal(barrier, 1, device_id=(dom, lat + 1), device_id_type=MESH)

    row = lax.broadcasted_iota(jnp.int32, (48, 128), 0) - 16 + lat * 16
    cor[...] = (DT * ROT) * (2.0 * (row.astype(jnp.float32) + 0.5) / (lats * 16) - 1.0)

    @pl.when(lat == 0)
    def _():
        xs[:, :, pl.ds(0, 8), :] = jnp.zeros((2, 4, 8, W), jnp.float32)
        xs[:, 0, pl.ds(0, 8), :] = jnp.full((2, 8, W), DEPTH, jnp.float32)

    @pl.when(lat == lats - 1)
    def _():
        xs[:, :, pl.ds(24, 8), :] = jnp.zeros((2, 4, 8, W), jnp.float32)
        xs[:, 0, pl.ds(24, 8), :] = jnp.full((2, 8, W), DEPTH, jnp.float32)

    for c in loads:
        c.wait()
    def row_of(c, island):
        j0, j1 = anc[c, 0, island], anc[c, 1, island]
        keep = (j0 >= 2).astype(jnp.int32)
        return keep, jnp.where(j0 >= 2, j1, j0), jnp.where(j0 >= 2, j0, j1) - 2

    nxt, prv = (dom + 1) % islands, (dom + islands - 1) % islands
    o0, a0, _ = row_of(0, dom)
    o0p, _, _ = row_of(0, prv)
    _, _, b0n = row_of(0, nxt)
    o1, a1, b1 = row_of(1, dom)
    _, _, b1n = row_of(1, nxt)

    def choose(p, pick, rows):
        for f in range(3):
            raw = jnp.where(pick == 1, xr[f, 1, pl.ds(rows, 8), :], xr[f, 0, pl.ds(rows, 8), :])
            xs[p, f, pl.ds(8 + rows, 8), :] = raw * HALF if f else DEPTH + raw * DEPTH
        add = jnp.where(pick == 1, n0[1, pl.ds(rows, 8), :], n0[0, pl.ds(rows, 8), :])
        xs[p, 3, pl.ds(8 + rows, 8), :] = add * DEPTH

    for p, pick in ((0, b0n), (1, a0)):
        for rows in (0, 8):
            choose(p, pick, rows)

    pl.semaphore_wait(
        barrier, 7 + (lat > 0).astype(jnp.int32) + (lat < lats - 1).astype(jnp.int32)
    )

    def halo(d, p):
        s, t = (8, 24) if d == 0 else (16, 0)
        return pltpu.make_async_remote_copy(
            xs.at[p, :, pl.ds(s, 8)], xs.at[p, :, pl.ds(t, 8)], hsend.at[d, p], hrecv.at[d, p],
            device_id=(dom, lat - 1) if d == 0 else (dom, lat + 1), device_id_type=MESH,
        )

    for p in range(2):
        @pl.when(lat > 0)
        def _():
            halo(0, p).start()

        @pl.when(lat < lats - 1)
        def _():
            halo(1, p).start()

    def arrived_halo(p):
        @pl.when(lat < lats - 1)
        def _():
            halo(0, p).wait_recv()

        @pl.when(lat > 0)
        def _():
            halo(1, p).wait_recv()

    def masked(t, val, f):
        if t == 1:
            return jnp.where(lat > 0, val, REST[f])
        if t == 4:
            return jnp.where(lat < lats - 1, val, REST[f])
        return val

    def section(src, dst, old, tiles):
        for t in tiles:
            new = stage_tile(src, old, cor, t)
            for f in range(3):
                dst[f, pl.ds(8 * t, 8), :] = masked(t, new[f], f)

    def forecast(last):
        every = range(1, 5)
        section(a, b, None, every)
        section(b, a, a, every)
        section(a, b, None, every)
        section(b, a, a, range(2, 4) if last else every)

    def twice(p):
        arrived_halo(p)
        for t in range(1, 5):
            r = 8 * t
            for f in range(3):
                a[f, pl.ds(r, 8), :] = xs[p, f, pl.ds(r - 8, 8), :]
        forecast(False)
        for t in range(1, 5):
            r = 8 * t
            a[0, pl.ds(r, 8), :] = masked(t, a[0, pl.ds(r, 8), :] + xs[p, 3, pl.ds(r - 8, 8), :], 0)
        forecast(True)

    def send(d, n, k):
        src = own.at[d, k] if n == 1 else ring.at[d, n - 2, k]
        return pltpu.make_async_remote_copy(
            src, ring.at[d, n - 1, k], rsend.at[d, n - 1, k], rrecv.at[d, n - 1, k],
            device_id=hop(d, n), device_id_type=MESH,
        )

    def pass_on(d):
        return pltpu.make_async_remote_copy(
            own.at[d, pl.ds(0, 3)], byp.at[d], bsend.at[d], brecv.at[d],
            device_id=at(nxt_xy, z), device_id_type=MESH,
        )

    twice(0)
    for f in range(3):
        for d in range(2):
            own[d, f] = a[f, pl.ds(16 + 8 * d, 8), :]
            send(d, 1, f).start()
    for d in range(2):
        pass_on(d).start()

    twice(1)
    for d in range(2):
        rows = pl.ds(8 * d, 8)
        fh = a[0, pl.ds(16 + 8 * d, 8), :]
        foh[d] = fh
        own[d, 3] = jnp.where(b1n == o0, fh, 0.0) + DEPTH * jnp.where(b1n == 1, n1[1, rows, :], n1[0, rows, :])
        send(d, 1, 3).start()
    for f in range(1, 3):
        for d in range(2):
            own[d, 3 + f] = a[f, pl.ds(16 + 8 * d, 8), :]
            send(d, 1, 3 + f).start()

    for n in range(2, HOPS + 1):
        for k in range(6):
            for d in range(2):
                send(d, n - 1, k).wait_recv()
                send(d, n, k).start()

    @pl.when(lat > 0)
    def _():
        for p in range(2):
            halo(0, p).wait_send()

    @pl.when(lat < lats - 1)
    def _():
        for p in range(2):
            halo(1, p).wait_send()

    for d in range(2):
        pass_on(d).wait()
    for n in range(1, HOPS):
        for k in range(6):
            for d in range(2):
                send(d, n, k).wait_send()

    last = HOPS - 1

    def plain(f, v):
        return v * (1.0 / HALF) if f else v * (1.0 / DEPTH) - 1.0

    def put(f, d, va, vb):
        rows = pl.ds(8 * d, 8)
        out[f, 0, rows, :] = jnp.where(o1 == 0, va, vb)
        out[f, 1, rows, :] = jnp.where(o1 == 0, vb, va)

    for k in range(3):
        for d in range(2):
            send(d, HOPS, k).wait_recv()
    for f in range(3):
        for d in range(2):
            rows = pl.ds(8 * d, 8)
            mine = foh[d] if f == 0 else own[d, 3 + f]
            va = jnp.where(a1 == o0, mine, ring[d, last, f])
            if f == 0:
                va = va + DEPTH * jnp.where(a1 == 1, n1[1, rows, :], n1[0, rows, :])
            send(d, HOPS, 3 + f).wait_recv()
            arrived = ring[d, last, 3 + f]
            if f == 0:
                vb = arrived + jnp.where(b1 == o0p, 0.0, byp[d, 0])
            else:
                vb = jnp.where(b1 == o0p, arrived, byp[d, f])
            put(f, d, plain(f, va), plain(f, vb))
    for k in range(6):
        for d in range(2):
            send(d, HOPS, k).wait_send()


def solution(mesh):
    islands, lats = mesh.shape["dom"], mesh.shape["lat"]

    def body(states, stir_noise, ancestors):
        f32 = jnp.float32
        dma = pltpu.SemaphoreType.DMA
        return pl.pallas_call(
            functools.partial(kernel, islands, lats),
            out_shape=jax.ShapeDtypeStruct(states.shape, f32),
            in_specs=[
                pl.BlockSpec(memory_space=pltpu.HBM),
                pl.BlockSpec(memory_space=pltpu.HBM),
                pl.BlockSpec(memory_space=pltpu.HBM),
            ],
            out_specs=pl.BlockSpec(memory_space=pltpu.VMEM),
            scratch_shapes=[
                pltpu.SMEM((2, 2, islands), jnp.int32),
                pltpu.VMEM((3, 2, 16, W), f32),
                pltpu.VMEM((2, 16, W), f32),
                pltpu.VMEM((2, 4, 32, W), f32),
                pltpu.VMEM((2, 16, W), f32),
                pltpu.VMEM((3, 48, W), f32),
                pltpu.VMEM((3, 48, W), f32),
                pltpu.VMEM((48, 128), f32),
                pltpu.VMEM((2, 6, 8, W), f32),
                pltpu.VMEM((2, 8, W), f32),
                pltpu.VMEM((2, HOPS, 6, 8, W), f32),
                pltpu.VMEM((2, 3, 8, W), f32),
                dma((4,)),
                dma((2, 2)),
                dma((2, 2)),
                dma((2, HOPS, 6)),
                dma((2, HOPS, 6)),
                dma((2,)),
                dma((2,)),
            ],
            compiler_params=pltpu.CompilerParams(collective_id=0, has_side_effects=True, vmem_limit_bytes=20 * 2**20),
            name="filter_ring",
        )(*(pltpu.with_memory_space_constraint(v, pltpu.HBM) for v in (jnp.transpose(ancestors, (0, 2, 1)), states, stir_noise)))

    spec = P(None, "dom", "lat", None)
    return jax.shard_map(body, mesh=mesh, in_specs=(spec, spec, P()), out_specs=spec, check_vma=False)
```

```python
import functools

import jax
import jax.numpy as jnp
from jax import lax
from jax.experimental import pallas as pl
from jax.experimental.pallas import tpu as pltpu
from jax.sharding import PartitionSpec as P

MESH = pl.DeviceIdType.MESH
DT = 0.2
HALF = 0.5 * DT
NU = 0.05 * DT
DEPTH = HALF * HALF
REST = (DEPTH, 0.0, 0.0)
ROT = 0.3
W = 1024
HOPS = 8
SIDE = 4


def terms(h, u, v, hs, us, vs, cor):
    he, hw, hn, hb = hs
    ue, uw, un, ub = us
    ve, vw, vn, vb = vs
    keep = 1.0 - 4.0 * NU
    lh = (he + hw) + (hn + hb)
    lu = (ue + uw) + (un + ub)
    lv = (ve + vw) + (vn + vb)
    return (
        h * keep + NU * lh - ((he * ue - hw * uw) + (hn * vn - hb * vb)),
        u * (keep - (ue - uw)) + v * (cor - (un - ub)) + (NU * lu - (he - hw)),
        v * (keep - (vn - vb)) - u * (cor + (ve - vw)) + (NU * lv - (hn - hb)),
    )


def stage_tile(src, old, cor, t):
    r = 8 * t
    sub = lax.broadcasted_iota(jnp.int32, (8, W), 0)
    mid, shifts = [], []
    for f in range(3):
        c = src[f, pl.ds(r, 8), :]
        nxt = src[f, pl.ds(r + 8, 8), :]
        prv = src[f, pl.ds(r - 8, 8), :]
        mid.append(c)
        shifts.append(
            (
                pltpu.roll(c, W - 1, 1),
                pltpu.roll(c, 1, 1),
                pltpu.roll(jnp.where(sub == 0, nxt, c), 7, 0),
                pltpu.roll(jnp.where(sub == 7, prv, c), 1, 0),
            )
        )
    cr = jnp.broadcast_to(cor[pl.ds(r, 8), 0:1], (8, W))
    new = terms(*mid, *shifts, cr)
    if old is None:
        return new
    return tuple(0.5 * (old[f, pl.ds(r, 8), :] + new[f]) for f in range(3))


def kernel(
    islands, lats, parents, states, noise, out, anc, xr, n0, xs, n1, a, b, cor, own, foh, ring, byp,
    lsem, hsend, hrecv, rsend, rrecv, bsend, brecv,
):
    dom, lat = lax.axis_index("dom"), lax.axis_index("lat")
    columns = islands // 2
    half = lats // 2
    depth = 2 * half
    xy, core = dom // 2, lat % 2
    z = (dom % 2) * half + lat // 2

    def at(xy_, z_):
        return (xy_ * 2 + z_ // half, (z_ % half) * 2 + core)

    zs = ((z + 1) % depth, (z + depth - 1) % depth)
    nxt_xy, prv_xy = (xy + 1) % columns, (xy + columns - 1) % columns
    side = SIDE
    x, y = xy // side, xy % side
    east = x * side + (y + 1) % side
    west = x * side + (y + side - 1) % side
    over = (xy + side) % columns
    under = (xy + columns - side) % columns

    def hop(d, n):
        origin = (z + depth - (n - 1)) % depth if d == 0 else (z + n - 1) % depth
        high = origin // half
        to = xy
        if n == 4:
            to = high * east + (1 - high) * xy
        if n == 5:
            wrap = high * (y == 0).astype(jnp.int32)
            to = wrap * over + (1 - wrap) * xy
        return at(to, zs[d])

    loads = [
        pltpu.make_async_copy(states, xr, lsem.at[0]),
        pltpu.make_async_copy(noise.at[0], n0, lsem.at[1]),
        pltpu.make_async_copy(noise.at[1], n1, lsem.at[2]),
        pltpu.make_async_copy(parents, anc, lsem.at[3]),
    ]
    for c in loads:
        c.start()

    barrier = pltpu.get_barrier_semaphore()
    for d in range(2):
        for col in (xy, west):
            pl.semaphore_signal(barrier, 1, device_id=at(col, zs[d]), device_id_type=MESH)

    @pl.when(y == 0)
    def _():
        for d in range(2):
            pl.semaphore_signal(barrier, 1, device_id=at(under, zs[d]), device_id_type=MESH)

    pl.semaphore_signal(barrier, 1, device_id=at(prv_xy, z), device_id_type=MESH)

    @pl.when(lat > 0)
    def _():
        pl.semaphore_signal(barrier, 1, device_id=(dom, lat - 1), device_id_type=MESH)

    @pl.when(lat < lats - 1)
    def _():
        pl.semaphore_signal(barrier, 1, device_id=(dom, lat + 1), device_id_type=MESH)

    row = lax.broadcasted_iota(jnp.int32, (48, 128), 0) - 16 + lat * 16
    cor[...] = (DT * ROT) * (2.0 * (row.astype(jnp.float32) + 0.5) / (lats * 16) - 1.0)

    @pl.when(lat == 0)
    def _():
        xs[:, :, pl.ds(0, 8), :] = jnp.zeros((2, 4, 8, W), jnp.float32)
        xs[:, 0, pl.ds(0, 8), :] = jnp.full((2, 8, W), DEPTH, jnp.float32)

    @pl.when(lat == lats - 1)
    def _():
        xs[:, :, pl.ds(24, 8), :] = jnp.zeros((2, 4, 8, W), jnp.float32)
        xs[:, 0, pl.ds(24, 8), :] = jnp.full((2, 8, W), DEPTH, jnp.float32)

    for c in loads:
        c.wait()
    def row_of(c, island):
        j0, j1 = anc[c, 0, island], anc[c, 1, island]
        keep = (j0 >= 2).astype(jnp.int32)
        return keep, jnp.where(j0 >= 2, j1, j0), jnp.where(j0 >= 2, j0, j1) - 2

    nxt, prv = (dom + 1) % islands, (dom + islands - 1) % islands
    o0, a0, _ = row_of(0, dom)
    o0p, _, _ = row_of(0, prv)
    _, _, b0n = row_of(0, nxt)
    o1, a1, b1 = row_of(1, dom)
    _, _, b1n = row_of(1, nxt)

    def choose(p, pick, rows):
        for f in range(3):
            raw = jnp.where(pick == 1, xr[f, 1, pl.ds(rows, 8), :], xr[f, 0, pl.ds(rows, 8), :])
            xs[p, f, pl.ds(8 + rows, 8), :] = raw * HALF if f else DEPTH + raw * DEPTH
        add = jnp.where(pick == 1, n0[1, pl.ds(rows, 8), :], n0[0, pl.ds(rows, 8), :])
        xs[p, 3, pl.ds(8 + rows, 8), :] = add * DEPTH

    for p, pick in ((0, b0n), (1, a0)):
        for rows in (0, 8):
            choose(p, pick, rows)

    pl.semaphore_wait(
        barrier, 5 + 2 * (y == 0).astype(jnp.int32) + (lat > 0).astype(jnp.int32) + (lat < lats - 1).astype(jnp.int32)
    )

    def halo(d, p):
        s, t = (8, 24) if d == 0 else (16, 0)
        return pltpu.make_async_remote_copy(
            xs.at[p, :, pl.ds(s, 8)], xs.at[p, :, pl.ds(t, 8)], hsend.at[d, p], hrecv.at[d, p],
            device_id=(dom, lat - 1) if d == 0 else (dom, lat + 1), device_id_type=MESH,
        )

    for p in range(2):
        @pl.when(lat > 0)
        def _():
            halo(0, p).start()

        @pl.when(lat < lats - 1)
        def _():
            halo(1, p).start()

    def arrived_halo(p):
        @pl.when(lat < lats - 1)
        def _():
            halo(0, p).wait_recv()

        @pl.when(lat > 0)
        def _():
            halo(1, p).wait_recv()

    def masked(t, val, f):
        if t == 1:
            return jnp.where(lat > 0, val, REST[f])
        if t == 4:
            return jnp.where(lat < lats - 1, val, REST[f])
        return val

    def section(src, dst, old, tiles):
        for t in tiles:
            new = stage_tile(src, old, cor, t)
            for f in range(3):
                dst[f, pl.ds(8 * t, 8), :] = masked(t, new[f], f)

    def forecast(emit=None):
        every = range(1, 5)
        section(a, b, None, every)
        section(b, a, a, every)
        section(a, b, None, every)
        if emit is None:
            section(b, a, a, every)
        else:
            for d in range(2):
                emit(d, stage_tile(b, a, cor, 2 + d))

    def twice(p, emit):
        arrived_halo(p)
        for t in range(1, 5):
            r = 8 * t
            for f in range(3):
                a[f, pl.ds(r, 8), :] = xs[p, f, pl.ds(r - 8, 8), :]
        forecast()
        for t in range(1, 5):
            r = 8 * t
            a[0, pl.ds(r, 8), :] = masked(t, a[0, pl.ds(r, 8), :] + xs[p, 3, pl.ds(r - 8, 8), :], 0)
        forecast(emit)

    def send(d, n, k):
        src = own.at[d, k] if n == 1 else ring.at[d, n - 2, k]
        return pltpu.make_async_remote_copy(
            src, ring.at[d, n - 1, k], rsend.at[d, n - 1, k], rrecv.at[d, n - 1, k],
            device_id=hop(d, n), device_id_type=MESH,
        )

    def pass_on(d):
        return pltpu.make_async_remote_copy(
            own.at[d, pl.ds(0, 3)], byp.at[d], bsend.at[d], brecv.at[d],
            device_id=at(nxt_xy, z), device_id_type=MESH,
        )

    def emit_first(d, new):
        for f in range(3):
            own[d, f] = new[f]
            send(d, 1, f).start()

    def emit_second(d, new):
        rows = pl.ds(8 * d, 8)
        foh[d] = new[0]
        own[d, 3] = jnp.where(b1n == o0, new[0], 0.0) + DEPTH * jnp.where(b1n == 1, n1[1, rows, :], n1[0, rows, :])
        own[d, 4] = new[1]
        own[d, 5] = new[2]
        for k in range(3, 6):
            send(d, 1, k).start()

    twice(0, emit_first)
    for d in range(2):
        pass_on(d).start()
    twice(1, emit_second)

    for n in range(2, HOPS + 1):
        for k in range(6):
            for d in range(2):
                send(d, n - 1, k).wait_recv()
                send(d, n, k).start()

    @pl.when(lat > 0)
    def _():
        for p in range(2):
            halo(0, p).wait_send()

    @pl.when(lat < lats - 1)
    def _():
        for p in range(2):
            halo(1, p).wait_send()

    for d in range(2):
        pass_on(d).wait()
    for n in range(1, HOPS):
        for k in range(6):
            for d in range(2):
                send(d, n, k).wait_send()

    last = HOPS - 1

    def plain(f, v):
        return v * (1.0 / HALF) if f else v * (1.0 / DEPTH) - 1.0

    def put(f, d, va, vb):
        rows = pl.ds(8 * d, 8)
        out[f, 0, rows, :] = jnp.where(o1 == 0, va, vb)
        out[f, 1, rows, :] = jnp.where(o1 == 0, vb, va)

    for k in range(3):
        for d in range(2):
            send(d, HOPS, k).wait_recv()
    for f in range(3):
        for d in range(2):
            rows = pl.ds(8 * d, 8)
            mine = foh[d] if f == 0 else own[d, 3 + f]
            va = jnp.where(a1 == o0, mine, ring[d, last, f])
            if f == 0:
                va = va + DEPTH * jnp.where(a1 == 1, n1[1, rows, :], n1[0, rows, :])
            send(d, HOPS, 3 + f).wait_recv()
            arrived = ring[d, last, 3 + f]
            if f == 0:
                vb = arrived + jnp.where(b1 == o0p, 0.0, byp[d, 0])
            else:
                vb = jnp.where(b1 == o0p, arrived, byp[d, f])
            put(f, d, plain(f, va), plain(f, vb))
    for k in range(6):
        for d in range(2):
            send(d, HOPS, k).wait_send()


def solution(mesh):
    islands, lats = mesh.shape["dom"], mesh.shape["lat"]

    def body(states, stir_noise, ancestors):
        f32 = jnp.float32
        dma = pltpu.SemaphoreType.DMA
        return pl.pallas_call(
            functools.partial(kernel, islands, lats),
            out_shape=jax.ShapeDtypeStruct(states.shape, f32),
            in_specs=[
                pl.BlockSpec(memory_space=pltpu.HBM),
                pl.BlockSpec(memory_space=pltpu.HBM),
                pl.BlockSpec(memory_space=pltpu.HBM),
            ],
            out_specs=pl.BlockSpec(memory_space=pltpu.VMEM),
            scratch_shapes=[
                pltpu.SMEM((2, 2, islands), jnp.int32),
                pltpu.VMEM((3, 2, 16, W), f32),
                pltpu.VMEM((2, 16, W), f32),
                pltpu.VMEM((2, 4, 32, W), f32),
                pltpu.VMEM((2, 16, W), f32),
                pltpu.VMEM((3, 48, W), f32),
                pltpu.VMEM((3, 48, W), f32),
                pltpu.VMEM((48, 128), f32),
                pltpu.VMEM((2, 6, 8, W), f32),
                pltpu.VMEM((2, 8, W), f32),
                pltpu.VMEM((2, HOPS, 6, 8, W), f32),
                pltpu.VMEM((2, 3, 8, W), f32),
                dma((4,)),
                dma((2, 2)),
                dma((2, 2)),
                dma((2, HOPS, 6)),
                dma((2, HOPS, 6)),
                dma((2,)),
                dma((2,)),
            ],
            compiler_params=pltpu.CompilerParams(collective_id=0, has_side_effects=True, vmem_limit_bytes=20 * 2**20),
            name="filter_ring",
        )(*(pltpu.with_memory_space_constraint(v, pltpu.HBM) for v in (jnp.transpose(ancestors, (0, 2, 1)), states, stir_noise)))

    spec = P(None, "dom", "lat", None)
    return jax.shard_map(body, mesh=mesh, in_specs=(spec, spec, P()), out_specs=spec, check_vma=False)
```
